512 devices in a mesh: dp: 128 (over z, y, core), mp: 4 (over x).
Axes of the slice: x: 4, y: 4, z: 16, core: 2. Of those that a mesh axis runs over, the one named last changes fastest.
Arguments:
- features: bfloat16 [8192, 4096], P('dp', 'mp'), may hold values from -6 to 6
- norm_gain: bfloat16 [4096], replicated, may hold values from 0.099609375 to 1.8984375
- w_key: bfloat16 [4096, 512], P('dp', 'mp'), may hold values from -0.09375 to 0.09375
- w_value: bfloat16 [4096, 512], P('dp', 'mp'), may hold values from -0.09375 to 0.09375
- queries: bfloat16 [8192, 2048], P('dp', 'mp'), may hold values from -150 to 150
- key_pool: bfloat16 [256, 128, 512], P('dp', None, 'mp'), may hold values from -5 to 5
- value_pool: bfloat16 [256, 128, 512], P('dp', None, 'mp'), may hold values from -5 to 5
- cache_lens: int32 [3], replicated, may hold values from 2 to 15360, as said below
- page_table: int32 [3, 186], replicated, may hold values from -1 to 255, as said below
- token_request: int32 [8192], replicated, may hold values from 0 to 2, as said below
Outputs:
- attended: bfloat16 [8192, 2048], P('dp', 'mp')
- keys_out: bfloat16 [256, 128, 512], P('dp', None, 'mp')
- values_out: bfloat16 [256, 128, 512], P('dp', None, 'mp')
The draws below stay inside these ranges and needn't reach their ends.
Inputs may be any that keep to these rules, and one draw needn't show every extreme that they name: `cache_lens`: exactly one request has 15360 cached tokens, each other request has at most 512. `page_table`: row r lists the pool pages of request r in logical order: its first ceil(cache_lens[r] / 128) entries are pages among the first 1 slots of some device, the entries up to the page of its last new token are pages among the other slots of some device, later entries are -1; no pool page is listed twice. `token_request`: never falling along the new tokens; every request has 2048 or more new tokens.
All inputs are finite; a program needn't handle non-finite values.
Results may differ from the reference program's by a relative error of at most 0.0068.
Values may be sent and summed in bfloat16 or wider, within the bound.
A program may use at most 64 MiB of HBM per device.

```python
import math
import jax
import jax.numpy as jnp
from jax import lax

D = 4096
HD = 128
HQ = 16
KVH = 4
PAGE = 128
SHORT = 512
REQS = 3
NEW = 8192
CTX = 15360
OLD_DEV = 1
NEW_DEV = 1
PAGES_DEV = 2
POOL = 256
SLOTS_OLD = 128
SLOTS_NEW = 128
MAXP = 186


def plan_requests(key):
    base = jax.random.fold_in(key, 11)
    key_list = jax.random.split(base, 6)
    first_size = jax.random.randint(key_list[0], (), NEW // 4, NEW // 3 + 1, dtype=jnp.int32)
    second_size = jax.random.randint(key_list[1], (), NEW // 4, NEW // 3 + 1, dtype=jnp.int32)
    third_size = NEW - first_size - second_size
    block_sizes = jnp.stack([first_size, second_size, third_size]).astype(jnp.int32)
    longest = jax.random.randint(key_list[2], (), 0, REQS, dtype=jnp.int32)
    shorts = jax.random.randint(key_list[3], (REQS,), 2, SHORT + 1, dtype=jnp.int32)
    lengths = jnp.where(jnp.arange(REQS, dtype=jnp.int32) == longest, CTX, shorts).astype(jnp.int32)
    old_count = (lengths + PAGE - 1) // PAGE
    all_count = (lengths + block_sizes + PAGE - 1) // PAGE
    fresh_count = all_count - old_count
    old_ids = jnp.arange(SLOTS_OLD, dtype=jnp.int32)
    old_pages = jax.random.permutation(key_list[4], old_ids // OLD_DEV * PAGES_DEV + old_ids % OLD_DEV)
    fresh_ids = jnp.arange(SLOTS_NEW, dtype=jnp.int32)
    fresh_pages = jax.random.permutation(key_list[5], fresh_ids // NEW_DEV * PAGES_DEV + OLD_DEV + fresh_ids % NEW_DEV)
    top_page = jnp.max(fresh_pages).astype(jnp.int32)
    top_at = jnp.argmax(fresh_pages).astype(jnp.int32)
    first_page = fresh_pages[0]
    fresh_pages = fresh_pages.at[top_at].set(first_page).at[0].set(top_page).astype(jnp.int32)
    old_start = jnp.cumsum(old_count).astype(jnp.int32) - old_count
    fresh_start = jnp.cumsum(fresh_count).astype(jnp.int32) - fresh_count
    logical = jnp.arange(MAXP, dtype=jnp.int32)[None, :]
    old_pick = jnp.take(old_pages, jnp.clip(old_start[:, None] + logical, 0, SLOTS_OLD - 1))
    fresh_pick = jnp.take(fresh_pages, jnp.clip(fresh_start[:, None] + logical - old_count[:, None], 0, SLOTS_NEW - 1))
    page_map = jnp.where(logical < old_count[:, None], old_pick, jnp.where(logical < all_count[:, None], fresh_pick, -1)).astype(jnp.int32)
    token_ids = jnp.arange(NEW, dtype=jnp.int32)
    request_map = ((token_ids >= first_size).astype(jnp.int32) + (token_ids >= first_size + second_size).astype(jnp.int32)).astype(jnp.int32)
    return (lengths, page_map, request_map)


def pool_keys(key):
    values = jnp.clip(jax.random.normal(jax.random.fold_in(key, 21), (POOL, PAGE, KVH * HD), jnp.float32), -5.0, 5.0)
    return values


def draw_cache_lens(key, part):
    return plan_requests(key)[0]


def draw_page_table(key, part):
    return plan_requests(key)[1]


def draw_token_request(key, part):
    return plan_requests(key)[2]


def draw_key_pool(key, part):
    return pool_keys(key).astype(jnp.bfloat16)


def draw_queries(key, part):
    values = jnp.clip(jax.random.normal(jax.random.fold_in(key, 31), (NEW, HQ * HD), jnp.float32), -5.0, 5.0)
    return values.astype(jnp.bfloat16)


def block_scale(own_key, dims, cuts, smallest, top_value):
    def one(axis_at, parts):
        steps = jax.random.uniform(jax.random.fold_in(jax.random.fold_in(own_key, 6), axis_at), (parts,), jnp.float32, smallest / len(cuts), top_value / len(cuts))
        return jnp.repeat(jnp.exp(steps), dims[axis_at] // parts).reshape((-1,) + (1,) * (len(dims) - axis_at - 1))

    level = one(*cuts[0])
    for cut in cuts[1:]:
        level = level * one(*cut)
    return level


def scatter_about(key, dims, scale, bound, shards=(), kind=jnp.bfloat16):
    loudness = block_scale(key, dims, shards, -0.22, 0.18) if shards else 1.0
    values = jax.random.normal(key, dims, jnp.float32) * scale * loudness
    return jnp.minimum(jnp.maximum(values, -bound), bound).astype(kind)


def setup_inputs(seed: int = 0) -> dict:
    key_of = jax.random.split(jax.random.key(seed), 11)
    features = scatter_about(key_of[0], (NEW, D), 1.0, 6.0, ((0, 128), (1, 4)))
    norm_gain = jnp.clip(1.0 + 0.18 * jax.random.normal(key_of[1], (D,), jnp.float32), 0.099609375, 1.8984375).astype(jnp.bfloat16)
    w_key = scatter_about(key_of[2], (D, KVH * HD), D ** -0.5, 0.09375, ((0, 128), (1, 4)))
    w_value = scatter_about(key_of[3], (D, KVH * HD), D ** -0.5, 0.09375, ((0, 128), (1, 4)))
    queries = draw_queries(jax.random.fold_in(key_of[10], 71), 0)
    key_pool = draw_key_pool(jax.random.fold_in(key_of[10], 71), 0)
    value_pool = scatter_about(key_of[6], (POOL, PAGE, KVH * HD), 1.0, 5.0, ((0, 128), (2, 4)))
    cache_lens = draw_cache_lens(jax.random.fold_in(key_of[10], 71), 0)
    page_table = draw_page_table(jax.random.fold_in(key_of[10], 71), 0)
    token_request = draw_token_request(jax.random.fold_in(key_of[10], 71), 0)
    return {"features": features, "norm_gain": norm_gain, "w_key": w_key, "w_value": w_value, "queries": queries, "key_pool": key_pool, "value_pool": value_pool, "cache_lens": cache_lens, "page_table": page_table, "token_request": token_request}


THETA = 500000.0

def rotate(values, positions, head_size):
    halfway = head_size // 2
    inverse = THETA ** (-(jnp.arange(halfway, dtype=jnp.float32) * 2.0) / head_size)
    angles = positions.astype(jnp.float32)[:, None] * inverse[None, :]
    cosine = jnp.cos(angles)[:, None, :]
    sine = jnp.sin(angles)[:, None, :]
    first_half = values[..., :halfway]
    second_half = values[..., halfway:]
    return jnp.concatenate([first_half * cosine - second_half * sine, second_half * cosine + first_half * sine], axis=-1)

def reference(features, norm_gain, w_key, w_value, queries, key_pool, value_pool, cache_lens, page_table, token_request):
    widened = features.astype(jnp.float32)
    mean_square = lax.optimization_barrier(jnp.mean(widened * widened, axis=1, keepdims=True))
    normed = (widened * lax.rsqrt(mean_square + 1e-05) * norm_gain.astype(jnp.float32)).astype(jnp.bfloat16)
    key_sums = jnp.dot(normed, w_key, preferred_element_type=jnp.float32)
    value_sums = jnp.dot(normed, w_value, preferred_element_type=jnp.float32)
    request_ids = jnp.arange(REQS, dtype=jnp.int32)
    member = (token_request[:, None] == request_ids[None, :]).astype(jnp.int32)
    counts = lax.optimization_barrier(jnp.sum(member, axis=0)).astype(jnp.int32)
    starts = (jnp.cumsum(counts) - counts).astype(jnp.int32)
    token_index = jnp.arange(NEW, dtype=jnp.int32)
    token_pos = (lax.optimization_barrier(jnp.sum(member * (cache_lens - starts)[None, :], axis=1)) + token_index).astype(jnp.int32)
    new_keys = rotate(key_sums.reshape(NEW, KVH, HD), token_pos, HD).reshape(NEW, KVH * HD).astype(jnp.bfloat16)
    new_values = value_sums.astype(jnp.bfloat16)
    slots = page_table[token_request, token_pos // PAGE].astype(jnp.int32)
    rows_in = (token_pos % PAGE).astype(jnp.int32)
    keys_out = key_pool.at[slots, rows_in].set(new_keys)
    values_out = value_pool.at[slots, rows_in].set(new_values)
    safe_pages = jnp.maximum(page_table, 0).astype(jnp.int32)
    logical_keys = keys_out[safe_pages].reshape(REQS, MAXP * PAGE, KVH, HD)
    logical_values = values_out[safe_pages].reshape(REQS, MAXP * PAGE, KVH, HD)
    key_limit = (cache_lens + counts).astype(jnp.int32)
    positions = jnp.arange(MAXP * PAGE, dtype=jnp.int32)
    group_size = HQ // KVH
    grouped = queries.reshape(NEW, KVH, group_size, HD)
    scale = 1.0 / math.sqrt(HD)
    block_rows = 128

    def one_block(block_start):
        block_queries = lax.dynamic_slice_in_dim(grouped, block_start, block_rows).astype(jnp.float32)
        block_request = lax.dynamic_slice_in_dim(token_request, block_start, block_rows)
        block_pos = lax.dynamic_slice_in_dim(token_pos, block_start, block_rows)
        result = jnp.zeros((block_rows, KVH, group_size, HD), jnp.float32)
        for which in range(REQS):

            def compute(current):
                keys_wide = logical_keys[which].astype(jnp.float32)
                values_wide = logical_values[which].astype(jnp.float32)
                scores = jnp.einsum('thgd,khd->thgk', block_queries, keys_wide) * scale
                visible = (positions[None, :] < key_limit[which]) & (positions[None, :] <= block_pos[:, None]) & (block_request[:, None] == which)
                mask_full = visible[:, None, None, :]
                masked = jnp.where(mask_full, scores, -jnp.inf)
                top_score = lax.optimization_barrier(jnp.max(masked, axis=-1, keepdims=True))
                top_score = jnp.where(jnp.isfinite(top_score), top_score, 0.0)
                weights = jnp.where(mask_full, jnp.exp(jnp.where(mask_full, scores - top_score, 0.0)), 0.0)
                total = lax.optimization_barrier(jnp.sum(weights, axis=-1))
                rounded = lax.optimization_barrier(weights.astype(jnp.bfloat16)).astype(jnp.float32)
                mixed = jnp.einsum('thgk,khd->thgd', rounded, values_wide)
                safe_total = jnp.where(total > 0.0, total, 1.0)
                piece_out = mixed / safe_total[..., None]
                return jnp.where((block_request == which)[:, None, None, None], piece_out, current)
            result = lax.cond(jnp.any(block_request == which), compute, lambda current: current, result)
        return result.astype(jnp.bfloat16)
    blocks_out = lax.map(one_block, jnp.arange(0, NEW, block_rows, dtype=jnp.int32))
    attended = blocks_out.reshape(NEW, HQ * HD)
    return (attended, keys_out, values_out)
```

```python
import math

import jax
import jax.numpy as jnp
from jax import lax
from jax.sharding import Mesh
from jax.sharding import PartitionSpec as P

HD = 128
OLD_DEV = 1
KEY_BLOCK = 2048

THETA = 500000.0
NEG_FILL = -1e30

ZY = ("z", "y")
ROWS = ("z", "y", "core")


def rotate(values, positions, head_size):
    halfway = head_size // 2
    inverse = THETA ** (-(jnp.arange(halfway, dtype=jnp.float32) * 2.0) / head_size)
    angles = positions.astype(jnp.float32)[:, None] * inverse[None, :]
    cosine = jnp.cos(angles)[:, None, :]
    sine = jnp.sin(angles)[:, None, :]
    first_half = values[..., :halfway]
    second_half = values[..., halfway:]
    return jnp.concatenate(
        [first_half * cosine - second_half * sine, second_half * cosine + first_half * sine],
        axis=-1,
    )


def gather_rows(payload):
    step = lax.all_gather(payload, ZY, axis=0, tiled=False)
    return lax.all_gather(step, "core", axis=0, tiled=False)


def make_body(n_zy, n_core):
    n_dp = n_zy * n_core

    def body(
        features,
        norm_gain,
        w_key,
        w_value,
        queries,
        key_pool,
        value_pool,
        cache_lens,
        page_table,
        token_request,
    ):
        tok_rows = features.shape[0]
        w_rows, kv_width = w_key.shape
        head_size = HD
        kv_heads = kv_width // head_size
        q_heads = queries.shape[1] // head_size
        group_size = q_heads // kv_heads
        scale = 1.0 / math.sqrt(head_size)
        pages_dev, page_rows, _ = key_pool.shape
        max_pages = page_table.shape[1]
        requests = cache_lens.shape[0]
        total_new = token_request.shape[0]

        core = lax.axis_index("core")
        zy = lax.axis_index("z") * (n_zy // lax.axis_size("z")) + lax.axis_index("y")
        dp_index = zy * n_core + core

        old_keys = key_pool[:OLD_DEV].reshape(OLD_DEV * page_rows, kv_width)
        old_values = value_pool[:OLD_DEV].reshape(OLD_DEV * page_rows, kv_width)
        first = gather_rows(jnp.concatenate([w_key, w_value, old_keys, old_values], axis=0))
        old_rows = OLD_DEV * page_rows
        wk_all = first[:, :, :w_rows].reshape(n_core * n_zy * w_rows, kv_width)
        wv_all = first[:, :, w_rows : 2 * w_rows].reshape(n_core * n_zy * w_rows, kv_width)
        cached_keys = first[:, :, 2 * w_rows : 2 * w_rows + old_rows].reshape(-1, kv_width)
        cached_values = first[:, :, 2 * w_rows + old_rows :].reshape(-1, kv_width)

        gathered = lax.all_gather(features, "x", axis=1, tiled=True)
        widened = gathered.astype(jnp.float32)
        mean_square = jnp.mean(widened * widened, axis=1, keepdims=True)
        normed = (
            widened * lax.rsqrt(mean_square + 1e-05) * norm_gain.astype(jnp.float32)
        ).astype(jnp.bfloat16)
        normed_cz = (
            normed.reshape(tok_rows, n_zy, n_core, w_rows)
            .transpose(0, 2, 1, 3)
            .reshape(tok_rows, -1)
        )
        key_sums = jnp.dot(normed_cz, wk_all, preferred_element_type=jnp.float32)
        value_sums = jnp.dot(normed_cz, wv_all, preferred_element_type=jnp.float32)

        request_ids = jnp.arange(requests, dtype=jnp.int32)
        member = (token_request[:, None] == request_ids[None, :]).astype(jnp.int32)
        counts = jnp.sum(member, axis=0)
        starts = jnp.cumsum(counts) - counts
        token_index = jnp.arange(total_new, dtype=jnp.int32)
        token_pos = jnp.sum(member * (cache_lens - starts)[None, :], axis=1) + token_index
        first_token = dp_index * tok_rows
        my_request = lax.dynamic_slice_in_dim(token_request, first_token, tok_rows)
        my_pos = lax.dynamic_slice_in_dim(token_pos, first_token, tok_rows)
        key_heads = rotate(key_sums.reshape(tok_rows, kv_heads, head_size), my_pos, head_size)
        new_keys = key_heads.reshape(tok_rows, kv_width).astype(jnp.bfloat16)
        new_values = value_sums.astype(jnp.bfloat16)

        page_core = jnp.arange(n_core, dtype=jnp.int32)[:, None]
        page_zy = jnp.arange(n_zy, dtype=jnp.int32)[None, :]
        slot_ids = jnp.arange(OLD_DEV, dtype=jnp.int32)[None, None, :]
        old_phys = ((page_zy * n_core + page_core)[:, :, None] * pages_dev + slot_ids).reshape(-1)
        matches = (page_table[None, :, :] == old_phys[:, None, None]).astype(jnp.int32)
        page_has = jnp.sum(matches, axis=(1, 2)) > 0
        page_request = jnp.sum(matches * request_ids[None, :, None], axis=(1, 2))
        page_logical = jnp.sum(
            matches * jnp.arange(max_pages, dtype=jnp.int32)[None, None, :], axis=(1, 2)
        )
        page_limit = jnp.sum(matches * cache_lens[None, :, None], axis=(1, 2))
        q_local = queries.reshape(tok_rows, kv_heads, group_size, head_size)

        def attend(att_state, keys_flat, values_flat, key_info):
            key_request, key_pos, key_ok = key_info
            visible = (
                key_ok[None, :]
                & (key_request[None, :] == my_request[:, None])
                & (key_pos[None, :] <= my_pos[:, None])
            )
            keys_shaped = keys_flat.reshape(keys_flat.shape[0], kv_heads, head_size)
            values_shaped = values_flat.reshape(values_flat.shape[0], kv_heads, head_size)
            running_max, running_sum, running_acc = att_state
            scores = (
                jnp.einsum(
                    "thgd,khd->thgk", q_local, keys_shaped, preferred_element_type=jnp.float32
                )
                * scale
            )
            mask_full = visible[:, None, None, :]
            masked = jnp.where(mask_full, scores, NEG_FILL)
            new_max = jnp.maximum(running_max, jnp.max(masked, axis=-1))
            factor = jnp.exp(running_max - new_max)
            soft_weights = jnp.where(mask_full, jnp.exp(masked - new_max[..., None]), 0.0)
            new_sum = running_sum * factor + jnp.sum(soft_weights, axis=-1)
            new_acc = running_acc * factor[..., None] + jnp.einsum(
                "thgk,khd->thgd",
                soft_weights.astype(jnp.bfloat16),
                values_shaped,
                preferred_element_type=jnp.float32,
            )
            return (new_max, new_sum, new_acc)

        def attend_rows(att_state, keys_flat, values_flat, key_info):
            row_count = keys_flat.shape[0]
            blocks = row_count // KEY_BLOCK
            stacked = (
                keys_flat.reshape(blocks, KEY_BLOCK, kv_width),
                values_flat.reshape(blocks, KEY_BLOCK, kv_width),
                key_info[0].reshape(blocks, KEY_BLOCK),
                key_info[1].reshape(blocks, KEY_BLOCK),
                key_info[2].reshape(blocks, KEY_BLOCK),
            )

            def step_block(inner_state, slab_parts):
                return (
                    attend(
                        inner_state,
                        slab_parts[0],
                        slab_parts[1],
                        (slab_parts[2], slab_parts[3], slab_parts[4]),
                    ),
                    None,
                )

            att_state, unused = lax.scan(step_block, att_state, stacked)
            return att_state

        start_state = (
            jnp.full((tok_rows, kv_heads, group_size), NEG_FILL, jnp.float32),
            jnp.zeros((tok_rows, kv_heads, group_size), jnp.float32),
            jnp.zeros((tok_rows, kv_heads, group_size, head_size), jnp.float32),
        )
        page_count = old_phys.shape[0]
        row_ids = jnp.arange(page_rows, dtype=jnp.int32)[None, :]
        key_pos = page_logical[:, None] * page_rows + row_ids
        key_ok = page_has[:, None] & (key_pos < page_limit[:, None])
        key_request = jnp.broadcast_to(page_request[:, None], (page_count, page_rows))
        middle_state = attend_rows(
            start_state,
            cached_keys,
            cached_values,
            (key_request.reshape(-1), key_pos.reshape(-1), key_ok.reshape(-1)),
        )

        second = gather_rows(jnp.concatenate([new_keys, new_values], axis=1))
        fresh = second.reshape(n_core * n_zy * tok_rows, 2 * kv_width)
        fresh_keys = fresh[:, :kv_width]
        fresh_values = fresh[:, kv_width:]
        fresh_request = (
            token_request.reshape(n_zy, n_core, tok_rows).transpose(1, 0, 2).reshape(-1)
        )
        fresh_pos = token_pos.reshape(n_zy, n_core, tok_rows).transpose(1, 0, 2).reshape(-1)
        att_state = attend_rows(
            middle_state,
            fresh_keys,
            fresh_values,
            (fresh_request, fresh_pos, jnp.ones((total_new,), jnp.bool_)),
        )
        final_max, final_sum, final_acc = att_state
        attended = (
            (final_acc / final_sum[..., None])
            .reshape(tok_rows, q_heads * head_size)
            .astype(jnp.bfloat16)
        )

        own_pages = dp_index * pages_dev + jnp.arange(pages_dev, dtype=jnp.int32)
        own_match = (page_table[None, :, :] == own_pages[:, None, None]).astype(jnp.int32)
        own_has = jnp.sum(own_match, axis=(1, 2)) > 0
        own_request = jnp.sum(own_match * request_ids[None, :, None], axis=(1, 2))
        own_logical = jnp.sum(
            own_match * jnp.arange(max_pages, dtype=jnp.int32)[None, None, :], axis=(1, 2)
        )
        row_pos = own_logical[:, None] * page_rows + row_ids
        lo = jnp.take(cache_lens, own_request)[:, None]
        hi = lo + jnp.take(counts, own_request)[:, None]
        row_new = own_has[:, None] & (row_pos >= lo) & (row_pos < hi)
        row_token = jnp.clip(jnp.take(starts, own_request)[:, None] + row_pos - lo, 0, total_new - 1)
        token_dp = row_token // tok_rows
        fresh_row = ((token_dp % n_core) * n_zy + token_dp // n_core) * tok_rows + row_token % tok_rows
        picked = jnp.take(fresh, fresh_row.reshape(-1), axis=0)
        row_new = row_new.reshape(-1, 1)
        flat_keys = key_pool.reshape(pages_dev * page_rows, kv_width)
        flat_values = value_pool.reshape(pages_dev * page_rows, kv_width)
        keys_out = jnp.where(row_new, picked[:, :kv_width], flat_keys)
        values_out = jnp.where(row_new, picked[:, kv_width:], flat_values)
        return (attended, keys_out.reshape(key_pool.shape), values_out.reshape(value_pool.shape))

    return body


def solution(mesh):
    n_dp, n_mp = mesh.devices.shape
    n_core = 2
    n_y = 4
    n_z = n_dp // (n_y * n_core)
    fine = Mesh(mesh.devices.reshape(n_z, n_y, n_core, n_mp), ("z", "y", "core", "x"))
    in_specs = (
        P(ROWS, "x"),
        P(),
        P(ROWS, "x"),
        P(ROWS, "x"),
        P(ROWS, "x"),
        P(ROWS, None, "x"),
        P(ROWS, None, "x"),
        P(),
        P(),
        P(),
    )
    out_specs = (P(ROWS, "x"), P(ROWS, None, "x"), P(ROWS, None, "x"))
    return jax.shard_map(
        make_body(n_z * n_y, n_core),
        mesh=fine,
        in_specs=in_specs,
        out_specs=out_specs,
        check_vma=False,
    )
```

```python
import math

import jax
import jax.numpy as jnp
from jax import lax
from jax.sharding import Mesh
from jax.sharding import PartitionSpec as P

HD = 128
OLD_DEV = 1
KEY_BLOCK = 2048

THETA = 500000.0
NEG_FILL = -1e30

ZY = ("z", "y")
ROWS = ("z", "y", "core")


def rotate(values, positions, head_size):
    halfway = head_size // 2
    inverse = THETA ** (-(jnp.arange(halfway, dtype=jnp.float32) * 2.0) / head_size)
    angles = positions.astype(jnp.float32)[:, None] * inverse[None, :]
    cosine = jnp.cos(angles)[:, None, :]
    sine = jnp.sin(angles)[:, None, :]
    first_half = values[..., :halfway]
    second_half = values[..., halfway:]
    return jnp.concatenate(
        [first_half * cosine - second_half * sine, second_half * cosine + first_half * sine],
        axis=-1,
    )


def gather_rows(payload):
    step = lax.all_gather(payload, "y", axis=0, tiled=False)
    step = lax.all_gather(step, "z", axis=0, tiled=False)
    shape = step.shape
    step = step.reshape((shape[0] * shape[1],) + shape[2:])
    return lax.all_gather(step, "core", axis=0, tiled=False)


def make_body(n_zy, n_core):
    n_dp = n_zy * n_core

    def body(
        features,
        norm_gain,
        w_key,
        w_value,
        queries,
        key_pool,
        value_pool,
        cache_lens,
        page_table,
        token_request,
    ):
        tok_rows = features.shape[0]
        w_rows, kv_width = w_key.shape
        head_size = HD
        kv_heads = kv_width // head_size
        q_heads = queries.shape[1] // head_size
        group_size = q_heads // kv_heads
        scale = 1.0 / math.sqrt(head_size)
        pages_dev, page_rows, _ = key_pool.shape
        max_pages = page_table.shape[1]
        requests = cache_lens.shape[0]
        total_new = token_request.shape[0]

        core = lax.axis_index("core")
        zy = lax.axis_index("z") * (n_zy // lax.axis_size("z")) + lax.axis_index("y")
        dp_index = zy * n_core + core

        old_keys = key_pool[:OLD_DEV].reshape(OLD_DEV * page_rows, kv_width)
        old_values = value_pool[:OLD_DEV].reshape(OLD_DEV * page_rows, kv_width)
        first = gather_rows(jnp.concatenate([w_key, w_value, old_keys, old_values], axis=0))
        old_rows = OLD_DEV * page_rows
        wk_all = first[:, :, :w_rows].reshape(n_core * n_zy * w_rows, kv_width)
        wv_all = first[:, :, w_rows : 2 * w_rows].reshape(n_core * n_zy * w_rows, kv_width)
        cached_keys = first[:, :, 2 * w_rows : 2 * w_rows + old_rows].reshape(-1, kv_width)
        cached_values = first[:, :, 2 * w_rows + old_rows :].reshape(-1, kv_width)

        gathered = lax.all_gather(features, "x", axis=1, tiled=True)
        widened = gathered.astype(jnp.float32)
        mean_square = jnp.mean(widened * widened, axis=1, keepdims=True)
        normed = (
            widened * lax.rsqrt(mean_square + 1e-05) * norm_gain.astype(jnp.float32)
        ).astype(jnp.bfloat16)
        normed_cz = (
            normed.reshape(tok_rows, n_zy, n_core, w_rows)
            .transpose(0, 2, 1, 3)
            .reshape(tok_rows, -1)
        )
        key_sums = jnp.dot(normed_cz, wk_all, preferred_element_type=jnp.float32)
        value_sums = jnp.dot(normed_cz, wv_all, preferred_element_type=jnp.float32)

        request_ids = jnp.arange(requests, dtype=jnp.int32)
        member = (token_request[:, None] == request_ids[None, :]).astype(jnp.int32)
        counts = jnp.sum(member, axis=0)
        starts = jnp.cumsum(counts) - counts
        token_index = jnp.arange(total_new, dtype=jnp.int32)
        token_pos = jnp.sum(member * (cache_lens - starts)[None, :], axis=1) + token_index
        first_token = dp_index * tok_rows
        my_request = lax.dynamic_slice_in_dim(token_request, first_token, tok_rows)
        my_pos = lax.dynamic_slice_in_dim(token_pos, first_token, tok_rows)
        key_heads = rotate(key_sums.reshape(tok_rows, kv_heads, head_size), my_pos, head_size)
        new_keys = key_heads.reshape(tok_rows, kv_width).astype(jnp.bfloat16)
        new_values = value_sums.astype(jnp.bfloat16)

        page_core = jnp.arange(n_core, dtype=jnp.int32)[:, None]
        page_zy = jnp.arange(n_zy, dtype=jnp.int32)[None, :]
        slot_ids = jnp.arange(OLD_DEV, dtype=jnp.int32)[None, None, :]
        old_phys = ((page_zy * n_core + page_core)[:, :, None] * pages_dev + slot_ids).reshape(-1)
        matches = (page_table[None, :, :] == old_phys[:, None, None]).astype(jnp.int32)
        page_has = jnp.sum(matches, axis=(1, 2)) > 0
        page_request = jnp.sum(matches * request_ids[None, :, None], axis=(1, 2))
        page_logical = jnp.sum(
            matches * jnp.arange(max_pages, dtype=jnp.int32)[None, None, :], axis=(1, 2)
        )
        page_limit = jnp.sum(matches * cache_lens[None, :, None], axis=(1, 2))
        q_local = queries.reshape(tok_rows, kv_heads, group_size, head_size)

        def attend(att_state, keys_flat, values_flat, key_info):
            key_request, key_pos, key_ok = key_info
            visible = (
                key_ok[None, :]
                & (key_request[None, :] == my_request[:, None])
                & (key_pos[None, :] <= my_pos[:, None])
            )
            keys_shaped = keys_flat.reshape(keys_flat.shape[0], kv_heads, head_size)
            values_shaped = values_flat.reshape(values_flat.shape[0], kv_heads, head_size)
            running_max, running_sum, running_acc = att_state
            scores = (
                jnp.einsum(
                    "thgd,khd->thgk", q_local, keys_shaped, preferred_element_type=jnp.float32
                )
                * scale
            )
            mask_full = visible[:, None, None, :]
            masked = jnp.where(mask_full, scores, NEG_FILL)
            new_max = jnp.maximum(running_max, jnp.max(masked, axis=-1))
            factor = jnp.exp(running_max - new_max)
            soft_weights = jnp.where(mask_full, jnp.exp(masked - new_max[..., None]), 0.0)
            new_sum = running_sum * factor + jnp.sum(soft_weights, axis=-1)
            new_acc = running_acc * factor[..., None] + jnp.einsum(
                "thgk,khd->thgd",
                soft_weights.astype(jnp.bfloat16),
                values_shaped,
                preferred_element_type=jnp.float32,
            )
            return (new_max, new_sum, new_acc)

        def attend_rows(att_state, keys_flat, values_flat, key_info):
            row_count = keys_flat.shape[0]
            blocks = row_count // KEY_BLOCK
            stacked = (
                keys_flat.reshape(blocks, KEY_BLOCK, kv_width),
                values_flat.reshape(blocks, KEY_BLOCK, kv_width),
                key_info[0].reshape(blocks, KEY_BLOCK),
                key_info[1].reshape(blocks, KEY_BLOCK),
                key_info[2].reshape(blocks, KEY_BLOCK),
            )

            def step_block(inner_state, slab_parts):
                return (
                    attend(
                        inner_state,
                        slab_parts[0],
                        slab_parts[1],
                        (slab_parts[2], slab_parts[3], slab_parts[4]),
                    ),
                    None,
                )

            att_state, unused = lax.scan(step_block, att_state, stacked)
            return att_state

        start_state = (
            jnp.full((tok_rows, kv_heads, group_size), NEG_FILL, jnp.float32),
            jnp.zeros((tok_rows, kv_heads, group_size), jnp.float32),
            jnp.zeros((tok_rows, kv_heads, group_size, head_size), jnp.float32),
        )
        page_count = old_phys.shape[0]
        row_ids = jnp.arange(page_rows, dtype=jnp.int32)[None, :]
        key_pos = page_logical[:, None] * page_rows + row_ids
        key_ok = page_has[:, None] & (key_pos < page_limit[:, None])
        key_request = jnp.broadcast_to(page_request[:, None], (page_count, page_rows))
        middle_state = attend_rows(
            start_state,
            cached_keys,
            cached_values,
            (key_request.reshape(-1), key_pos.reshape(-1), key_ok.reshape(-1)),
        )

        second = gather_rows(jnp.concatenate([new_keys, new_values], axis=1))
        fresh = second.reshape(n_core * n_zy * tok_rows, 2 * kv_width)
        fresh_keys = fresh[:, :kv_width]
        fresh_values = fresh[:, kv_width:]
        fresh_request = (
            token_request.reshape(n_zy, n_core, tok_rows).transpose(1, 0, 2).reshape(-1)
        )
        fresh_pos = token_pos.reshape(n_zy, n_core, tok_rows).transpose(1, 0, 2).reshape(-1)
        att_state = attend_rows(
            middle_state,
            fresh_keys,
            fresh_values,
            (fresh_request, fresh_pos, jnp.ones((total_new,), jnp.bool_)),
        )
        final_max, final_sum, final_acc = att_state
        attended = (
            (final_acc / final_sum[..., None])
            .reshape(tok_rows, q_heads * head_size)
            .astype(jnp.bfloat16)
        )

        own_pages = dp_index * pages_dev + jnp.arange(pages_dev, dtype=jnp.int32)
        own_match = (page_table[None, :, :] == own_pages[:, None, None]).astype(jnp.int32)
        own_has = jnp.sum(own_match, axis=(1, 2)) > 0
        own_request = jnp.sum(own_match * request_ids[None, :, None], axis=(1, 2))
        own_logical = jnp.sum(
            own_match * jnp.arange(max_pages, dtype=jnp.int32)[None, None, :], axis=(1, 2)
        )
        row_pos = own_logical[:, None] * page_rows + row_ids
        lo = jnp.take(cache_lens, own_request)[:, None]
        hi = lo + jnp.take(counts, own_request)[:, None]
        row_new = own_has[:, None] & (row_pos >= lo) & (row_pos < hi)
        row_token = jnp.clip(jnp.take(starts, own_request)[:, None] + row_pos - lo, 0, total_new - 1)
        token_dp = row_token // tok_rows
        fresh_row = ((token_dp % n_core) * n_zy + token_dp // n_core) * tok_rows + row_token % tok_rows
        picked = jnp.take(fresh, fresh_row.reshape(-1), axis=0)
        row_new = row_new.reshape(-1, 1)
        flat_keys = key_pool.reshape(pages_dev * page_rows, kv_width)
        flat_values = value_pool.reshape(pages_dev * page_rows, kv_width)
        keys_out = jnp.where(row_new, picked[:, :kv_width], flat_keys)
        values_out = jnp.where(row_new, picked[:, kv_width:], flat_values)
        return (attended, keys_out.reshape(key_pool.shape), values_out.reshape(value_pool.shape))

    return body


def solution(mesh):
    n_dp, n_mp = mesh.devices.shape
    n_core = 2
    n_y = 4
    n_z = n_dp // (n_y * n_core)
    fine = Mesh(mesh.devices.reshape(n_z, n_y, n_core, n_mp), ("z", "y", "core", "x"))
    in_specs = (
        P(ROWS, "x"),
        P(),
        P(ROWS, "x"),
        P(ROWS, "x"),
        P(ROWS, "x"),
        P(ROWS, None, "x"),
        P(ROWS, None, "x"),
        P(),
        P(),
        P(),
    )
    out_specs = (P(ROWS, "x"), P(ROWS, None, "x"), P(ROWS, None, "x"))
    return jax.shard_map(
        make_body(n_z * n_y, n_core),
        mesh=fine,
        in_specs=in_specs,
        out_specs=out_specs,
        check_vma=False,
    )
```
